32 devices in a mesh: img: 4 (over y, x), tpl: 8 (over z, core).
Axes of the slice: x: 2, y: 2, z: 4, core: 2. Of those that a mesh axis runs over, the one named last changes fastest.
Arguments:
- images: bfloat16 [6144, 2048], P(('img', 'tpl')), may hold values from -320 to 320
- templates: bfloat16 [3072, 2048], P('tpl'), may hold values from -0.62 to 0.62
- class_exponent: int32 [8], replicated, may hold values from 0 to 5
- class_mask: int32 [6144, 8], P('img'), may hold values from 0 to 1, as said below
Outputs:
- new_templates: float32 [3072, 2048], P('tpl', 'img')
- log_evidence: float32 [6144], P('img')
The draws below stay inside these ranges and needn't reach their ends.
Inputs may be any that keep to these rules, and one draw needn't show every extreme that they name: `class_mask`: every image is compared with at least one class.
All inputs are finite; a program needn't handle non-finite values.
Results may differ from the reference program's by a relative error of at most 0.0023.
Values may be sent and summed in bfloat16 or wider, within the bound.
A program may use at most 64 MiB of HBM per device.

```python
import math
import jax
import jax.numpy as jnp
from jax import lax

F = 2048
CLASSES = 8
IMG_DEV = 1536
IMAGES = 6144
TEMPLATES = 3072
N_IMG = 4


def shared_draw(key):
    key_base = jax.random.fold_in(key, 101)
    key_scale = jax.random.fold_in(key, 102)
    key_pics = jax.random.fold_in(key, 103)
    key_rows = jax.random.fold_in(key, 104)
    base = jnp.clip(jax.random.normal(key_base, (TEMPLATES, F), jnp.float32), -5.0, 5.0)
    tpl_scale = jnp.exp(jax.random.uniform(key_scale, (TEMPLATES, 1), jnp.float32, math.log(0.03), math.log(0.1)))
    pictures = jnp.clip(jax.random.normal(key_pics, (IMAGES, F), jnp.float32), -5.0, 5.0)
    pic_scale = jnp.exp(jax.random.uniform(key_rows, (IMAGES, 1), jnp.float32, math.log(0.5), math.log(2.0)))
    return (base, base * tpl_scale, pictures * pic_scale)


def aligned_draw(base, tmpl, pictures):
    picks = (jnp.arange(8, dtype=jnp.int32) * (TEMPLATES // 8)).astype(jnp.int32)
    rows = base[picks]
    signs = jnp.where(rows >= 0.0, 1.0, -1.0)
    leading = 0.12 * signs * (1.0 + jnp.minimum(jnp.abs(rows), 4.0))
    tmpl = tmpl.at[picks].set(leading).at[picks + 1].set(1.02 * leading)
    targets = (jnp.arange(8, dtype=jnp.int32) * (IMAGES // 8) + 3).astype(jnp.int32)
    factors = jnp.array([6.0, 8.0, 10.0, 12.0, 6.0, 8.0, 10.0, 12.0], jnp.float32)
    norms = jnp.sum(leading * leading, axis=1, keepdims=True)
    gains = 40.0 * factors[:, None] / norms
    pictures = pictures.at[targets].set(gains * leading)
    return (tmpl, pictures)


def draw_images(key, part):
    base, tmpl, pictures = shared_draw(key)
    tmpl, pictures = aligned_draw(base, tmpl, pictures)
    return pictures.astype(jnp.bfloat16)


def draw_templates(key, part):
    base, tmpl, pictures = shared_draw(key)
    tmpl, pictures = aligned_draw(base, tmpl, pictures)
    return tmpl.astype(jnp.bfloat16)


def draw_class_mask(key, part):
    key_bits = jax.random.fold_in(key, 201)
    key_force = jax.random.fold_in(key, 202)
    chosen = jax.random.randint(key_bits, (IMAGES, CLASSES), 0, 4) > 0
    forced = jax.random.randint(key_force, (IMAGES,), 0, CLASSES)
    forced_hit = jnp.arange(CLASSES, dtype=jnp.int32)[None, :] == forced[:, None]
    return jnp.logical_or(chosen, forced_hit).astype(jnp.int32)


def plant(drawn, key, least, high):
    longest = drawn.shape.index(max(drawn.shape))
    spots = []
    for shift in (0, 1):
        where = [jax.random.randint(jax.random.fold_in(key, axis), (), 0, length) for axis, length in enumerate(drawn.shape)]
        where[longest] = (where[longest] + shift) % drawn.shape[longest]
        spots.append(tuple(where))
    return drawn.at[spots[0]].set(least).at[spots[1]].set(high)


def setup_inputs(seed: int = 0) -> dict:
    keys = jax.random.split(jax.random.key(seed), 5)
    return {
        "images": draw_images(jax.random.fold_in(keys[4], 71), 0),
        "templates": draw_templates(jax.random.fold_in(keys[4], 71), 0),
        "class_exponent": plant(jax.random.randint(keys[2], (CLASSES,), 0, 6), jax.random.fold_in(keys[2], 1), 0, 5).astype(jnp.int32),
        "class_mask": draw_class_mask(jax.random.fold_in(keys[4], 71), 0),
    }


floor_score = -1.0e30


def reference(images, templates, class_exponent, class_mask):
    total_rows = templates.shape[0]
    per_class = total_rows // CLASSES
    template_f32 = templates.astype(jnp.float32)
    squared_norm = jnp.sum(template_f32 * template_f32, axis=1)
    owner = (jnp.arange(total_rows, dtype=jnp.int32) // per_class).astype(jnp.int32)
    inverse_temp = 0.5 * jnp.exp2(0.5 * class_exponent.astype(jnp.float32))
    beta = inverse_temp[owner]
    picture_blocks = images.reshape(N_IMG, IMG_DEV, F)
    mask_blocks = class_mask.reshape(N_IMG, IMG_DEV, CLASSES)

    def block_step(carry, item):
        pictures, allow_rows = item
        raw = jnp.dot(pictures, templates.T, preferred_element_type=jnp.float32)
        scores = beta[None, :] * (raw - 0.5 * squared_norm[None, :])
        allowed = allow_rows[:, owner] > 0
        top = jnp.max(jnp.where(allowed, scores, floor_score), axis=1, keepdims=True)
        expo = jnp.where(allowed, jnp.exp(scores - top), 0.0)
        totals = jnp.sum(expo, axis=1, keepdims=True)
        posterior = expo / totals
        weighted = carry[0] + jnp.dot(posterior.astype(jnp.bfloat16).T, pictures, preferred_element_type=jnp.float32)
        occupancy = carry[1] + jnp.sum(posterior, axis=0)
        return (weighted, occupancy), (top + jnp.log(totals))[:, 0]

    start = (jnp.zeros((total_rows, F), jnp.float32), jnp.zeros((total_rows,), jnp.float32))
    (weighted, occupancy), evidence = lax.scan(block_step, start, (picture_blocks, mask_blocks))
    new_templates = (weighted + template_f32) / (occupancy[:, None] + 1.0)
    return new_templates, evidence.reshape(-1)
```

```python
import functools

import jax
import jax.numpy as jnp
from jax import lax
from jax.experimental import pallas as pl
from jax.experimental.pallas import tpu as pltpu
from jax.sharding import PartitionSpec as P

MESH = pl.DeviceIdType.MESH
floor_score = -1e30


def kernel(
    n_img, n_tpl, x_ref, t_ref, beta_ref, mask_ref, out_ref, le_ref,
    imgs, e_ref, post_ref, st, acc, own, sbuf, rbuf, sqn, occ, obuf, orecv,
    img_send, img_recv, st_send, st_recv, rs_send, rs_recv, oc_send, oc_recv,
):
    chips = n_tpl // 2
    rows, feats = x_ref.shape
    cols = feats // n_img
    me_i, me_t = lax.axis_index("img"), lax.axis_index("tpl")
    chip, core = lax.div(me_t, 2), lax.rem(me_t, 2)
    sibling = 2 * chip + 1 - core

    def tpl_peer(off):
        return lax.rem(me_t + off, n_tpl)

    def img_peer(off):
        return lax.rem(me_i + off, n_img)

    barrier = pltpu.get_barrier_semaphore()
    for off in range(1, n_tpl):
        pl.semaphore_signal(barrier, inc=1, device_id={"tpl": tpl_peer(off)}, device_id_type=MESH)
    for off in range(1, n_img):
        pl.semaphore_signal(barrier, inc=1, device_id={"img": img_peer(off)}, device_id_type=MESH)
    pl.semaphore_wait(barrier, n_tpl - 1 + n_img - 1)

    def image_copy(src, block, way, to):
        return pltpu.make_async_remote_copy(
            src_ref=src, dst_ref=imgs.at[block], send_sem=img_send.at[way, lax.div(block, 2)],
            recv_sem=img_recv.at[block], device_id={"tpl": to}, device_id_type=MESH)

    right, left = me_t + 2, me_t - 2
    has_right, has_left = chip < chips - 1, chip > 0

    def forward(src, q):
        block = 2 * q + core

        @pl.when(jnp.logical_and(has_right, q <= chip))
        def _():
            image_copy(src, block, 0, right).start()

        @pl.when(jnp.logical_and(has_left, q >= chip))
        def _():
            image_copy(src, block, 1, left).start()

        image_copy(src, block, 2, sibling).start()

    forward(x_ref, chip)
    imgs[me_t] = x_ref[...]
    tf = t_ref[...].astype(jnp.float32)
    sqn[...] = 0.5 * jnp.sum(tf * tf, axis=1, keepdims=True)
    acc[...] = jnp.zeros_like(acc)
    occ[...] = jnp.zeros_like(occ)

    def stat_copy(q, off):
        return pltpu.make_async_remote_copy(
            src_ref=st.at[q, me_t], dst_ref=st.at[q, me_t], send_sem=st_send.at[q, off],
            recv_sem=st_recv.at[q, off], device_id={"tpl": tpl_peer(off)}, device_id_type=MESH)

    def stat_arrival(q, off):
        src = lax.rem(me_t + n_tpl - off, n_tpl)
        return pltpu.make_async_remote_copy(
            src_ref=st.at[q, src], dst_ref=st.at[q, src], send_sem=st_send.at[q, off],
            recv_sem=st_recv.at[q, off], device_id={"tpl": tpl_peer(off)}, device_id_type=MESH)

    def pair_of(q):
        return imgs[pl.ds(2 * q, 2)].reshape(2 * rows, feats)

    def score(q):
        raw = lax.dot_general(
            t_ref[...], pair_of(q), (((1,), (1,)), ((), ())), preferred_element_type=jnp.float32)
        s = beta_ref[...] * (raw - sqn[...])
        allowed = mask_ref[q] > 0.5
        top = jnp.max(jnp.where(allowed, s, floor_score), axis=0, keepdims=True)
        e = jnp.where(allowed, jnp.exp(s - top), 0.0)
        st[q, me_t, 0:1, :] = top
        st[q, me_t, 1:2, :] = jnp.sum(e, axis=0, keepdims=True)
        e_ref[q] = e
        for off in range(1, n_tpl):
            stat_copy(q, off).start()

    def wait_image(block):
        image_copy(imgs.at[block], block, 2, sibling).wait_recv()

    wait_image(2 * chip + 1 - core)
    score(chip)
    both = jnp.minimum(chip, chips - 1 - chip)

    def arrive(s, carry):
        near = lax.div(s + 1, 2)
        q_near = jnp.where(lax.rem(s, 2) == 1, chip - near, chip + near)
        far = s - both
        q_far = jnp.where(chip > chips - 1 - chip, chip - far, chip + far)
        q = jnp.where(s <= 2 * both, q_near, q_far)
        wait_image(2 * q + core)
        forward(imgs.at[2 * q + core], q)
        wait_image(2 * q + 1 - core)
        score(q)
        return carry

    lax.fori_loop(1, chips, arrive, 0)

    def consume(q):
        for off in range(1, n_tpl):
            stat_arrival(q, off).wait_recv()
        tops = [st[q, j, 0:1, :] for j in range(n_tpl)]
        top = functools.reduce(jnp.maximum, tops)
        total = sum(st[q, j, 1:2, :] * jnp.exp(tops[j] - top) for j in range(n_tpl))
        factor = jnp.exp(st[q, me_t, 0:1, :] - top) / total
        post = e_ref[q] * factor
        occ[...] += jnp.sum(post, axis=1, keepdims=True)
        post_ref[q] = post.astype(jnp.bfloat16)
        le_ref[q] = top + jnp.log(total)

    def middle(q, carry):
        consume(q)
        for j in range(n_img):
            part = slice(j * cols, (j + 1) * cols)
            block = imgs[pl.ds(2 * q, 2), :, part].reshape(2 * rows, cols)
            acc[:, part] += jnp.dot(post_ref[q], block, preferred_element_type=jnp.float32)
        return carry

    lax.fori_loop(1, chips - 1, middle, 0)
    ends = (0, chips - 1) if chips > 1 else (0,)
    for q in ends:
        consume(q)

    def occ_copy(off):
        return pltpu.make_async_remote_copy(
            src_ref=obuf, dst_ref=orecv.at[off], send_sem=oc_send.at[off],
            recv_sem=oc_recv.at[off], device_id={"img": img_peer(off)}, device_id_type=MESH)

    def sum_copy(off):
        return pltpu.make_async_remote_copy(
            src_ref=sbuf.at[off], dst_ref=rbuf.at[off], send_sem=rs_send.at[off],
            recv_sem=rs_recv.at[off], device_id={"img": img_peer(off)}, device_id_type=MESH)

    def share(off):
        part = pl.ds(pl.multiple_of(img_peer(off) * cols, cols), cols)
        value = acc[:, part]
        for q in ends:
            block = imgs[2 * q:2 * q + 2, :, part].reshape(2 * rows, cols)
            value += jnp.dot(post_ref[q], block, preferred_element_type=jnp.float32)
        return value

    tpl_rows = occ.shape[0]
    obuf[...] = jnp.transpose(jnp.broadcast_to(occ[...], (tpl_rows, 128)))[0:8]
    order = sorted(range(1, n_img), key=lambda off: abs(2 * off - n_img))
    for off in order:
        sbuf[off] = share(off).astype(jnp.bfloat16)
        sum_copy(off).start()
    for off in order:
        occ_copy(off).start()
    part = pl.ds(pl.multiple_of(me_i * cols, cols), cols)
    own[...] = share(0) + t_ref[:, part].astype(jnp.float32)
    occ_row = obuf[...]
    for off in range(1, n_img):
        occ_copy(off).wait_recv()
        occ_row += orecv[off]
    occ_col = jnp.transpose(jnp.broadcast_to(occ_row[0:1], (128, tpl_rows)))[:, 0:1]
    occ[...] = occ_col + 1.0
    total = own[...]
    for off in range(1, n_img):
        sum_copy(off).wait_recv()
        total += rbuf[off].astype(jnp.float32)
    out_ref[...] = total / occ[...]

    for off in range(1, n_img):
        occ_copy(off).wait_send()
        sum_copy(off).wait_send()

    def drain(q, carry):
        block = 2 * q + core

        @pl.when(jnp.logical_and(has_right, q <= chip))
        def _():
            image_copy(imgs.at[block], block, 0, right).wait_send()

        @pl.when(jnp.logical_and(has_left, q >= chip))
        def _():
            image_copy(imgs.at[block], block, 1, left).wait_send()

        image_copy(imgs.at[block], block, 2, sibling).wait_send()
        for off in range(1, n_tpl):
            stat_copy(q, off).wait_send()
        return carry

    lax.fori_loop(0, chips, drain, 0)


def solution(mesh):
    n_img, n_tpl = mesh.shape["img"], mesh.shape["tpl"]
    chips = n_tpl // 2

    def per_device(images, templates, class_exponent, class_mask):
        rows, feats = images.shape
        tpl_rows = templates.shape[0]
        cols = feats // n_img
        class_count = class_exponent.shape[0]
        per_class = tpl_rows * n_tpl // class_count
        first = lax.axis_index("tpl") * tpl_rows
        inverse_temp = 0.5 * jnp.exp2(0.5 * class_exponent.astype(jnp.float32))
        classes = jnp.arange(class_count, dtype=jnp.int32)
        owner = (first + jnp.arange(tpl_rows, dtype=jnp.int32)) // per_class
        onehot = (owner[:, None] == classes[None, :]).astype(jnp.float32)
        beta = jnp.sum(onehot * inverse_temp[None, :], axis=1, keepdims=True)
        if per_class % tpl_rows == 0:
            onehot = onehot[:1]
        mask = jnp.sum(jnp.where(onehot[:, :, None] > 0.5, class_mask.astype(jnp.float32).T[None], 0.0), axis=1)
        mask = mask.reshape(mask.shape[0], chips, 2 * rows).transpose(1, 0, 2)
        dma = pltpu.SemaphoreType.DMA
        vmem = pl.BlockSpec(memory_space=pltpu.VMEM)
        new, evidence = pl.pallas_call(
            functools.partial(kernel, n_img, n_tpl),
            out_shape=(
                jax.ShapeDtypeStruct((tpl_rows, cols), jnp.float32),
                jax.ShapeDtypeStruct((chips, 1, 2 * rows), jnp.float32),
            ),
            in_specs=[vmem] * 4,
            out_specs=(vmem, vmem),
            scratch_shapes=[
                pltpu.VMEM((n_tpl, rows, feats), jnp.bfloat16),
                pltpu.VMEM((chips, tpl_rows, 2 * rows), jnp.float32),
                pltpu.VMEM((chips, tpl_rows, 2 * rows), jnp.bfloat16),
                pltpu.VMEM((chips, n_tpl, 2, 2 * rows), jnp.float32),
                pltpu.VMEM((tpl_rows, feats), jnp.float32),
                pltpu.VMEM((tpl_rows, cols), jnp.float32),
                pltpu.VMEM((n_img, tpl_rows, cols), jnp.bfloat16),
                pltpu.VMEM((n_img, tpl_rows, cols), jnp.bfloat16),
                pltpu.VMEM((tpl_rows, 1), jnp.float32),
                pltpu.VMEM((tpl_rows, 1), jnp.float32),
                pltpu.VMEM((8, tpl_rows), jnp.float32),
                pltpu.VMEM((n_img, 8, tpl_rows), jnp.float32),
                dma((3, chips)),
                dma((n_tpl,)),
                dma((chips, n_tpl)),
                dma((chips, n_tpl)),
                dma((n_img,)),
                dma((n_img,)),
                dma((n_img,)),
                dma((n_img,)),
            ],
            compiler_params=pltpu.CompilerParams(
                collective_id=0, has_side_effects=True, vmem_limit_bytes=60 * 1024 * 1024),
        )(images, templates, beta, mask)
        return new, evidence.reshape(-1)

    in_specs = (P(("img", "tpl"), None), P("tpl", None), P(), P("img", None))
    out_specs = (P("tpl", "img"), P("img"))
    return jax.shard_map(
        per_device, mesh=mesh, in_specs=in_specs, out_specs=out_specs, check_vma=False
    )
```

```python
import functools

import jax
import jax.numpy as jnp
from jax import lax
from jax.experimental import pallas as pl
from jax.experimental.pallas import tpu as pltpu
from jax.sharding import PartitionSpec as P

MESH = pl.DeviceIdType.MESH
floor_score = -1e30


def kernel(
    n_img, n_tpl, parts, x_ref, t_ref, power_ref, mask_ref, out_ref, le_ref,
    imgs, allow, le_row, e_ref, post_ref, st, acc, own, sbuf, rbuf, sqn, occ, obuf, orecv,
    img_send, img_recv, st_send, st_recv, rs_send, rs_recv, oc_send, oc_recv,
):
    chips = n_tpl // 2
    rows, feats = x_ref.shape
    cols = feats // n_img
    me_i, me_t = lax.axis_index("img"), lax.axis_index("tpl")
    chip, core = lax.div(me_t, 2), lax.rem(me_t, 2)
    sibling = 2 * chip + 1 - core

    def tpl_peer(off):
        return lax.rem(me_t + off, n_tpl)

    def img_peer(off):
        return lax.rem(me_i + off, n_img)

    barrier = pltpu.get_barrier_semaphore()
    for off in range(1, n_tpl):
        pl.semaphore_signal(barrier, inc=1, device_id={"tpl": tpl_peer(off)}, device_id_type=MESH)
    for off in range(1, n_img):
        pl.semaphore_signal(barrier, inc=1, device_id={"img": img_peer(off)}, device_id_type=MESH)
    pl.semaphore_wait(barrier, n_tpl - 1 + n_img - 1)

    size = rows // parts

    def image_copy(src, block, k, way, to):
        piece = pl.ds(k * size, size)
        return pltpu.make_async_remote_copy(
            src_ref=src.at[piece], dst_ref=imgs.at[block, piece],
            send_sem=img_send.at[way, lax.div(block, 2), k],
            recv_sem=img_recv.at[block, k], device_id={"tpl": to}, device_id_type=MESH)

    right, left = me_t + 2, me_t - 2
    has_right, has_left = chip < chips - 1, chip > 0

    own_block = 2 * chip + core
    for k in range(parts):
        @pl.when(has_right)
        def _():
            image_copy(x_ref, own_block, k, 0, right).start()

        @pl.when(has_left)
        def _():
            image_copy(x_ref, own_block, k, 1, left).start()

        image_copy(x_ref, own_block, k, 2, sibling).start()

    imgs[me_t] = x_ref[...]
    tf = t_ref[...].astype(jnp.float32)
    sqn[...] = 0.5 * jnp.sum(tf * tf, axis=1, keepdims=True)
    acc[...] = jnp.zeros_like(acc)
    occ[...] = jnp.zeros_like(occ)

    def stat_copy(q, off):
        return pltpu.make_async_remote_copy(
            src_ref=st.at[q, me_t], dst_ref=st.at[q, me_t], send_sem=st_send.at[q, off],
            recv_sem=st_recv.at[q, off], device_id={"tpl": tpl_peer(off)}, device_id_type=MESH)

    def stat_arrival(q, off):
        src = lax.rem(me_t + n_tpl - off, n_tpl)
        return pltpu.make_async_remote_copy(
            src_ref=st.at[q, src], dst_ref=st.at[q, src], send_sem=st_send.at[q, off],
            recv_sem=st_recv.at[q, off], device_id={"tpl": tpl_peer(off)}, device_id_type=MESH)

    def pair_of(q):
        return imgs[pl.ds(2 * q, 2)].reshape(2 * rows, feats)

    class_count = power_ref.shape[0]
    tpl_rows = t_ref.shape[0]
    per_class = tpl_rows * n_tpl // class_count
    pair = 2 * rows
    first = me_t * tpl_rows
    for q in range(chips):
        allow[q] = mask_ref[:, q * pair:(q + 1) * pair]

    def inverse_temp(c):
        power = jnp.full((1, pair), power_ref[c], jnp.int32)
        return 0.5 * jnp.exp2(0.5 * power.astype(jnp.float32))

    if per_class % tpl_rows == 0:
        only = lax.div(first, per_class)
        beta = inverse_temp(only)

        def allowed_at(q):
            return allow[q, pl.ds(only, 1), :] > 0
    else:
        owner = lax.div(first + lax.broadcasted_iota(jnp.int32, (tpl_rows, pair), 0), per_class)
        beta = sum(jnp.where(owner == c, inverse_temp(c), 0.0) for c in range(class_count))

        def allowed_at(q):
            return sum(jnp.where(owner == c, allow[q, c:c + 1, :], 0) for c in range(class_count)) > 0

    def score(q):
        raw = lax.dot_general(
            t_ref[...], pair_of(q), (((1,), (1,)), ((), ())), preferred_element_type=jnp.float32)
        s = beta * (raw - sqn[...])
        allowed = allowed_at(q)
        top = jnp.max(jnp.where(allowed, s, floor_score), axis=0, keepdims=True)
        e = jnp.where(allowed, jnp.exp(s - top), 0.0)
        st[q, me_t, 0:1, :] = top
        st[q, me_t, 1:2, :] = jnp.sum(e, axis=0, keepdims=True)
        e_ref[q] = e
        for off in range(1, n_tpl):
            stat_copy(q, off).start()

    def wait_image(block, k):
        image_copy(imgs.at[block], block, k, 2, sibling).wait_recv()

    def relay(q, k, more, way, to):
        block = 2 * q + core
        wait_image(block, k)

        @pl.when(more)
        def _():
            image_copy(imgs.at[block], block, k, way, to).start()

        image_copy(imgs.at[block], block, k, 2, sibling).start()

    def finish(q):
        for k in range(parts):
            wait_image(2 * q + 1 - core, k)
        score(q)

    finish(chip)

    def arrive(d, carry):
        q_left, q_right = chip - d, chip + d
        for k in range(parts):
            @pl.when(q_left >= 0)
            def _():
                relay(q_left, k, has_right, 0, right)

            @pl.when(q_right < chips)
            def _():
                relay(q_right, k, has_left, 1, left)

        @pl.when(q_left >= 0)
        def _():
            finish(q_left)

        @pl.when(q_right < chips)
        def _():
            finish(q_right)

        return carry

    lax.fori_loop(1, chips, arrive, 0)

    def consume(q):
        for off in range(1, n_tpl):
            stat_arrival(q, off).wait_recv()
        tops = [st[q, j, 0:1, :] for j in range(n_tpl)]
        top = functools.reduce(jnp.maximum, tops)
        total = sum(st[q, j, 1:2, :] * jnp.exp(tops[j] - top) for j in range(n_tpl))
        factor = jnp.exp(st[q, me_t, 0:1, :] - top) / total
        post = e_ref[q] * factor
        occ[...] += jnp.sum(post, axis=1, keepdims=True)
        post_ref[q] = post.astype(jnp.bfloat16)
        le_row[q] = top + jnp.log(total)

    def middle(q, carry):
        consume(q)
        for j in range(n_img):
            part = slice(j * cols, (j + 1) * cols)
            block = imgs[pl.ds(2 * q, 2), :, part].reshape(2 * rows, cols)
            acc[:, part] += jnp.dot(post_ref[q], block, preferred_element_type=jnp.float32)
        return carry

    lax.fori_loop(1, chips - 1, middle, 0)
    ends = (0, chips - 1) if chips > 1 else (0,)
    for q in ends:
        consume(q)

    def occ_copy(off):
        return pltpu.make_async_remote_copy(
            src_ref=obuf, dst_ref=orecv.at[off], send_sem=oc_send.at[off],
            recv_sem=oc_recv.at[off], device_id={"img": img_peer(off)}, device_id_type=MESH)

    def sum_copy(off):
        return pltpu.make_async_remote_copy(
            src_ref=sbuf.at[off], dst_ref=rbuf.at[off], send_sem=rs_send.at[off],
            recv_sem=rs_recv.at[off], device_id={"img": img_peer(off)}, device_id_type=MESH)

    def share(off):
        part = pl.ds(pl.multiple_of(img_peer(off) * cols, cols), cols)
        value = acc[:, part]
        for q in ends:
            block = imgs[2 * q:2 * q + 2, :, part].reshape(2 * rows, cols)
            value += jnp.dot(post_ref[q], block, preferred_element_type=jnp.float32)
        return value

    for q in range(chips):
        le_ref[:, q * pair:(q + 1) * pair] = le_row[q]
    obuf[...] = jnp.transpose(jnp.broadcast_to(occ[...], (tpl_rows, 128)))[0:8]
    order = sorted(range(1, n_img), key=lambda off: abs(2 * off - n_img))
    for off in order:
        sbuf[off] = share(off).astype(jnp.bfloat16)
        sum_copy(off).start()
    for off in order:
        occ_copy(off).start()
    part = pl.ds(pl.multiple_of(me_i * cols, cols), cols)
    own[...] = share(0) + t_ref[:, part].astype(jnp.float32)
    occ_row = obuf[...]
    for off in range(1, n_img):
        occ_copy(off).wait_recv()
        occ_row += orecv[off]
    occ_col = jnp.transpose(jnp.broadcast_to(occ_row[0:1], (128, tpl_rows)))[:, 0:1]
    occ[...] = occ_col + 1.0
    total = own[...]
    for off in range(1, n_img):
        sum_copy(off).wait_recv()
        total += rbuf[off].astype(jnp.float32)
    out_ref[...] = total / occ[...]

    for off in range(1, n_img):
        occ_copy(off).wait_send()
        sum_copy(off).wait_send()

    def drain(q, carry):
        block = 2 * q + core
        for k in range(parts):
            @pl.when(jnp.logical_and(has_right, q <= chip))
            def _():
                image_copy(imgs.at[block], block, k, 0, right).wait_send()

            @pl.when(jnp.logical_and(has_left, q >= chip))
            def _():
                image_copy(imgs.at[block], block, k, 1, left).wait_send()

            image_copy(imgs.at[block], block, k, 2, sibling).wait_send()
        for off in range(1, n_tpl):
            stat_copy(q, off).wait_send()
        return carry

    lax.fori_loop(0, chips, drain, 0)


def solution(mesh):
    n_img, n_tpl = mesh.shape["img"], mesh.shape["tpl"]
    chips = n_tpl // 2

    def per_device(images, templates, class_exponent, class_mask):
        rows, feats = images.shape
        tpl_rows = templates.shape[0]
        cols = feats // n_img
        class_count = class_exponent.shape[0]
        parts = max(c for c in (4, 3, 2, 1) if rows % (16 * c) == 0 or c == 1)
        dma = pltpu.SemaphoreType.DMA
        vmem = pl.BlockSpec(memory_space=pltpu.VMEM)
        new, evidence = pl.pallas_call(
            functools.partial(kernel, n_img, n_tpl, parts),
            out_shape=(
                jax.ShapeDtypeStruct((tpl_rows, cols), jnp.float32),
                jax.ShapeDtypeStruct((1, n_tpl * rows), jnp.float32),
            ),
            in_specs=[vmem, vmem, pl.BlockSpec(memory_space=pltpu.SMEM), vmem],
            out_specs=(vmem, vmem),
            scratch_shapes=[
                pltpu.VMEM((n_tpl, rows, feats), jnp.bfloat16),
                pltpu.VMEM((chips, class_count, 2 * rows), jnp.int32),
                pltpu.VMEM((chips, 1, 2 * rows), jnp.float32),
                pltpu.VMEM((chips, tpl_rows, 2 * rows), jnp.float32),
                pltpu.VMEM((chips, tpl_rows, 2 * rows), jnp.bfloat16),
                pltpu.VMEM((chips, n_tpl, 2, 2 * rows), jnp.float32),
                pltpu.VMEM((tpl_rows, feats), jnp.float32),
                pltpu.VMEM((tpl_rows, cols), jnp.float32),
                pltpu.VMEM((n_img, tpl_rows, cols), jnp.bfloat16),
                pltpu.VMEM((n_img, tpl_rows, cols), jnp.bfloat16),
                pltpu.VMEM((tpl_rows, 1), jnp.float32),
                pltpu.VMEM((tpl_rows, 1), jnp.float32),
                pltpu.VMEM((8, tpl_rows), jnp.float32),
                pltpu.VMEM((n_img, 8, tpl_rows), jnp.float32),
                dma((3, chips, parts)),
                dma((n_tpl, parts)),
                dma((chips, n_tpl)),
                dma((chips, n_tpl)),
                dma((n_img,)),
                dma((n_img,)),
                dma((n_img,)),
                dma((n_img,)),
            ],
            compiler_params=pltpu.CompilerParams(
                collective_id=0, has_side_effects=True, vmem_limit_bytes=60 * 1024 * 1024),
        )(images, templates, class_exponent, class_mask.T)
        return new, evidence.reshape(-1)

    in_specs = (P(("img", "tpl"), None), P("tpl", None), P(), P("img", None))
    out_specs = (P("tpl", "img"), P("img"))
    return jax.shard_map(
        per_device, mesh=mesh, in_specs=in_specs, out_specs=out_specs, check_vma=False
    )
```

```python
import functools

import jax
import jax.numpy as jnp
from jax import lax
from jax.experimental import pallas as pl
from jax.experimental.pallas import tpu as pltpu
from jax.sharding import PartitionSpec as P

MESH = pl.DeviceIdType.MESH
floor_score = -1e30


def kernel(
    n_img, n_tpl, parts, x_ref, t_ref, power_ref, mask_ref, out_ref, le_ref,
    imgs, allow, le_row, e_ref, post_ref, st, acc, own, sbuf, rbuf, sqn, occ, obuf, orecv,
    img_send, img_recv, st_send, st_recv, rs_send, rs_recv, oc_send, oc_recv,
):
    chips = n_tpl // 2
    rows, feats = x_ref.shape
    cols = feats // n_img
    me_i, me_t = lax.axis_index("img"), lax.axis_index("tpl")
    chip, core = lax.div(me_t, 2), lax.rem(me_t, 2)
    sibling = 2 * chip + 1 - core

    def tpl_peer(off):
        return lax.rem(me_t + off, n_tpl)

    def img_peer(off):
        return lax.rem(me_i + off, n_img)

    barrier = pltpu.get_barrier_semaphore()
    for off in range(1, n_tpl):
        pl.semaphore_signal(barrier, inc=1, device_id={"tpl": tpl_peer(off)}, device_id_type=MESH)
    for off in range(1, n_img):
        pl.semaphore_signal(barrier, inc=1, device_id={"img": img_peer(off)}, device_id_type=MESH)
    pl.semaphore_wait(barrier, n_tpl - 1 + n_img - 1)

    size = rows // parts

    def image_copy(src, block, k, way, to):
        piece = pl.ds(k * size, size)
        return pltpu.make_async_remote_copy(
            src_ref=src.at[piece], dst_ref=imgs.at[block, piece],
            send_sem=img_send.at[way, lax.div(block, 2), k],
            recv_sem=img_recv.at[block, k], device_id={"tpl": to}, device_id_type=MESH)

    right, left = me_t + 2, me_t - 2
    has_right, has_left = chip < chips - 1, chip > 0

    own_block = 2 * chip + core
    for k in range(parts):
        @pl.when(has_right)
        def _():
            image_copy(x_ref, own_block, k, 0, right).start()

        @pl.when(has_left)
        def _():
            image_copy(x_ref, own_block, k, 1, left).start()

        image_copy(x_ref, own_block, k, 2, sibling).start()

    imgs[me_t] = x_ref[...]
    tf = t_ref[...].astype(jnp.float32)
    sqn[...] = 0.5 * jnp.sum(tf * tf, axis=1, keepdims=True)
    acc[...] = jnp.zeros_like(acc)
    occ[...] = jnp.zeros_like(occ)

    def stat_copy(q, off):
        return pltpu.make_async_remote_copy(
            src_ref=st.at[q, me_t], dst_ref=st.at[q, me_t], send_sem=st_send.at[q, off],
            recv_sem=st_recv.at[q, off], device_id={"tpl": tpl_peer(off)}, device_id_type=MESH)

    def stat_arrival(q, off):
        src = lax.rem(me_t + n_tpl - off, n_tpl)
        return pltpu.make_async_remote_copy(
            src_ref=st.at[q, src], dst_ref=st.at[q, src], send_sem=st_send.at[q, off],
            recv_sem=st_recv.at[q, off], device_id={"tpl": tpl_peer(off)}, device_id_type=MESH)

    def pair_of(q):
        return imgs[pl.ds(2 * q, 2)].reshape(2 * rows, feats)

    class_count = power_ref.shape[0]
    tpl_rows = t_ref.shape[0]
    per_class = tpl_rows * n_tpl // class_count
    pair = 2 * rows
    first = me_t * tpl_rows
    for q in range(chips):
        allow[q] = mask_ref[:, q * pair:(q + 1) * pair]

    def inverse_temp(c):
        power = jnp.full((1, pair), power_ref[c], jnp.int32)
        return 0.5 * jnp.exp2(0.5 * power.astype(jnp.float32))

    if per_class % tpl_rows == 0:
        only = lax.div(first, per_class)
        beta = inverse_temp(only)

        def allowed_at(q):
            return allow[q, pl.ds(only, 1), :] > 0
    else:
        owner = lax.div(first + lax.broadcasted_iota(jnp.int32, (tpl_rows, pair), 0), per_class)
        beta = sum(jnp.where(owner == c, inverse_temp(c), 0.0) for c in range(class_count))

        def allowed_at(q):
            return sum(jnp.where(owner == c, allow[q, c:c + 1, :], 0) for c in range(class_count)) > 0

    def score(q):
        raw = lax.dot_general(
            t_ref[...], pair_of(q), (((1,), (1,)), ((), ())), preferred_element_type=jnp.float32)
        s = beta * (raw - sqn[...])
        allowed = allowed_at(q)
        top = jnp.max(jnp.where(allowed, s, floor_score), axis=0, keepdims=True)
        e = jnp.where(allowed, jnp.exp(s - top), 0.0)
        st[q, me_t, 0:1, :] = top
        st[q, me_t, 1:2, :] = jnp.sum(e, axis=0, keepdims=True)
        e_ref[q] = e
        for off in range(1, n_tpl):
            stat_copy(q, off).start()

    def wait_image(block, k):
        image_copy(imgs.at[block], block, k, 2, sibling).wait_recv()

    def relay(q, k, more, way, to):
        block = 2 * q + core
        wait_image(block, k)

        @pl.when(more)
        def _():
            image_copy(imgs.at[block], block, k, way, to).start()

        image_copy(imgs.at[block], block, k, 2, sibling).start()

    def finish(q):
        for k in range(parts):
            wait_image(2 * q + 1 - core, k)
        score(q)

    finish(chip)

    def arrive(d, carry):
        q_left, q_right = chip - d, chip + d
        for k in range(parts):
            @pl.when(q_left >= 0)
            def _():
                relay(q_left, k, has_right, 0, right)

            @pl.when(q_right < chips)
            def _():
                relay(q_right, k, has_left, 1, left)

        @pl.when(q_left >= 0)
        def _():
            finish(q_left)

        @pl.when(q_right < chips)
        def _():
            finish(q_right)

        return carry

    lax.fori_loop(1, chips, arrive, 0)

    def consume(q):
        for off in range(1, n_tpl):
            stat_arrival(q, off).wait_recv()
        tops = [st[q, j, 0:1, :] for j in range(n_tpl)]
        top = functools.reduce(jnp.maximum, tops)
        total = sum(st[q, j, 1:2, :] * jnp.exp(tops[j] - top) for j in range(n_tpl))
        factor = jnp.exp(st[q, me_t, 0:1, :] - top) / total
        post = e_ref[q] * factor
        occ[...] += jnp.sum(post, axis=1, keepdims=True)
        post_ref[q] = post.astype(jnp.bfloat16)
        le_row[q] = top + jnp.log(total)

    def middle(q, carry):
        consume(q)
        for j in range(n_img):
            part = slice(j * cols, (j + 1) * cols)
            block = imgs[pl.ds(2 * q, 2), :, part].reshape(2 * rows, cols)
            acc[:, part] += jnp.dot(post_ref[q], block, preferred_element_type=jnp.float32)
        return carry

    lax.fori_loop(1, chips - 1, middle, 0)
    ends = (0, chips - 1) if chips > 1 else (0,)
    for q in ends:
        consume(q)

    def occ_copy(off):
        return pltpu.make_async_remote_copy(
            src_ref=obuf, dst_ref=orecv.at[off], send_sem=oc_send.at[off],
            recv_sem=oc_recv.at[off], device_id={"img": img_peer(off)}, device_id_type=MESH)

    bits = [1 << k for k in range(n_img.bit_length() - 1)]
    groups = len(bits) if bits and tpl_rows % (16 * len(bits)) == 0 else 1
    depth = tpl_rows // groups
    orders = [bits[g:] + bits[:g] for g in range(groups)]

    def flip(mask):
        return me_i + sum(b - 2 * b * lax.rem(lax.div(me_i, b), 2) for b in bits if b & mask)

    def turn(g, mask):
        return next(r for r, b in enumerate(orders[g]) if b & mask)

    def band(g):
        return slice(g * depth, (g + 1) * depth)

    def sum_copy(g, mask):
        return pltpu.make_async_remote_copy(
            src_ref=sbuf.at[mask, band(g)], dst_ref=rbuf.at[mask, band(g)],
            send_sem=rs_send.at[g, mask], recv_sem=rs_recv.at[g, mask],
            device_id={"img": flip(orders[g][turn(g, mask)])}, device_id_type=MESH)

    def share(g, mask):
        part = pl.ds(pl.multiple_of(flip(mask) * cols, cols), cols)
        value = acc[band(g), part]
        for q in ends:
            block = imgs[2 * q:2 * q + 2, :, part].reshape(2 * rows, cols)
            value += jnp.dot(post_ref[q, band(g)], block, preferred_element_type=jnp.float32)
        return value

    def received(g, mask, rounds):
        value = 0.0
        for b in orders[g][:rounds]:
            sum_copy(g, b + mask).wait_recv()
            value += rbuf[b + mask, band(g)].astype(jnp.float32)
        return value

    for q in range(chips):
        le_ref[:, q * pair:(q + 1) * pair] = le_row[q]
    obuf[...] = jnp.transpose(jnp.broadcast_to(occ[...], (tpl_rows, 128)))[0:8]
    for off in range(1, n_img):
        occ_copy(off).start()
    masks = sorted(range(1, n_img), key=lambda mask: -mask.bit_count())
    mine = pl.ds(pl.multiple_of(me_i * cols, cols), cols)
    for r in range(len(bits)):
        for mask in masks:
            for g in range(groups):
                if turn(g, mask) == r:
                    value = share(g, mask)
                    sbuf[mask, band(g)] = (value + received(g, mask, r)).astype(jnp.bfloat16)
                    sum_copy(g, mask).start()
        if r == 0:
            for g in range(groups):
                own[band(g)] = share(g, 0) + t_ref[band(g), mine].astype(jnp.float32)
            occ_row = obuf[...]
            for off in range(1, n_img):
                occ_copy(off).wait_recv()
                occ_row += orecv[off]
            occ_col = jnp.transpose(jnp.broadcast_to(occ_row[0:1], (128, tpl_rows)))[:, 0:1]
            occ[...] = occ_col + 1.0
    for g in range(groups):
        out_ref[band(g)] = (own[band(g)] + received(g, 0, len(bits))) / occ[band(g)]

    for off in range(1, n_img):
        occ_copy(off).wait_send()
        for g in range(groups):
            sum_copy(g, off).wait_send()

    def drain(q, carry):
        block = 2 * q + core
        for k in range(parts):
            @pl.when(jnp.logical_and(has_right, q <= chip))
            def _():
                image_copy(imgs.at[block], block, k, 0, right).wait_send()

            @pl.when(jnp.logical_and(has_left, q >= chip))
            def _():
                image_copy(imgs.at[block], block, k, 1, left).wait_send()

            image_copy(imgs.at[block], block, k, 2, sibling).wait_send()
        for off in range(1, n_tpl):
            stat_copy(q, off).wait_send()
        return carry

    lax.fori_loop(0, chips, drain, 0)


def emit(new_ref, evidence_ref, new_out, evidence_out):
    new_out[...] = new_ref[...]
    evidence_out[...] = evidence_ref[...].reshape(evidence_out.shape)


def solution(mesh):
    n_img, n_tpl = mesh.shape["img"], mesh.shape["tpl"]
    chips = n_tpl // 2

    def per_device(images, templates, class_exponent, class_mask):
        rows, feats = images.shape
        tpl_rows = templates.shape[0]
        cols = feats // n_img
        class_count = class_exponent.shape[0]
        parts = max(c for c in (4, 3, 2, 1) if rows % (16 * c) == 0 or c == 1)
        dma = pltpu.SemaphoreType.DMA
        vmem = pl.BlockSpec(memory_space=pltpu.VMEM)
        new, evidence = pl.pallas_call(
            functools.partial(kernel, n_img, n_tpl, parts),
            out_shape=(
                jax.ShapeDtypeStruct((tpl_rows, cols), jnp.float32),
                jax.ShapeDtypeStruct((1, n_tpl * rows), jnp.float32),
            ),
            in_specs=[vmem, vmem, pl.BlockSpec(memory_space=pltpu.SMEM), vmem],
            out_specs=(vmem, vmem),
            scratch_shapes=[
                pltpu.VMEM((n_tpl, rows, feats), jnp.bfloat16),
                pltpu.VMEM((chips, class_count, 2 * rows), jnp.int32),
                pltpu.VMEM((chips, 1, 2 * rows), jnp.float32),
                pltpu.VMEM((chips, tpl_rows, 2 * rows), jnp.float32),
                pltpu.VMEM((chips, tpl_rows, 2 * rows), jnp.bfloat16),
                pltpu.VMEM((chips, n_tpl, 2, 2 * rows), jnp.float32),
                pltpu.VMEM((tpl_rows, feats), jnp.float32),
                pltpu.VMEM((tpl_rows, cols), jnp.float32),
                pltpu.VMEM((n_img, tpl_rows, cols), jnp.bfloat16),
                pltpu.VMEM((n_img, tpl_rows, cols), jnp.bfloat16),
                pltpu.VMEM((tpl_rows, 1), jnp.float32),
                pltpu.VMEM((tpl_rows, 1), jnp.float32),
                pltpu.VMEM((8, tpl_rows), jnp.float32),
                pltpu.VMEM((n_img, 8, tpl_rows), jnp.float32),
                dma((3, chips, parts)),
                dma((n_tpl, parts)),
                dma((chips, n_tpl)),
                dma((chips, n_tpl)),
                dma((n_img, n_img)),
                dma((n_img, n_img)),
                dma((n_img,)),
                dma((n_img,)),
            ],
            compiler_params=pltpu.CompilerParams(
                collective_id=0, has_side_effects=True, vmem_limit_bytes=60 * 1024 * 1024),
        )(images, templates, class_exponent, class_mask.T)
        return pl.pallas_call(
            emit,
            out_shape=(
                jax.ShapeDtypeStruct(new.shape, jnp.float32),
                jax.ShapeDtypeStruct((n_tpl * rows,), jnp.float32),
            ),
            in_specs=[vmem] * 2,
            out_specs=(vmem, vmem),
        )(new, evidence)

    in_specs = (P(("img", "tpl"), None), P("tpl", None), P(), P("img", None))
    out_specs = (P("tpl", "img"), P("img"))
    return jax.shard_map(
        per_device, mesh=mesh, in_specs=in_specs, out_specs=out_specs, check_vma=False
    )
```

```python
import functools

import jax
import jax.numpy as jnp
from jax import lax
from jax.experimental import pallas as pl
from jax.experimental.pallas import tpu as pltpu
from jax.sharding import PartitionSpec as P

MESH = pl.DeviceIdType.MESH
floor_score = -1e30


def kernel(
    n_img, n_tpl, parts, x_ref, t_hbm, power_ref, mask_hbm, out_ref, le_ref,
    t_ref, mask_ref, loads, imgs, allow, le_row, e_ref, post_ref, st, acc, own, sbuf, rbuf, sqn, occ, obuf, orecv,
    img_send, img_recv, st_send, st_recv, rs_send, rs_recv, oc_send, oc_recv,
):
    chips = n_tpl // 2
    rows, feats = x_ref.shape
    cols = feats // n_img
    me_i, me_t = lax.axis_index("img"), lax.axis_index("tpl")
    chip, core = lax.div(me_t, 2), lax.rem(me_t, 2)
    sibling = 2 * chip + 1 - core

    def tpl_peer(off):
        return lax.rem(me_t + off, n_tpl)

    def img_peer(off):
        return lax.rem(me_i + off, n_img)

    barrier = pltpu.get_barrier_semaphore()
    for off in range(1, n_tpl):
        pl.semaphore_signal(barrier, inc=1, device_id={"tpl": tpl_peer(off)}, device_id_type=MESH)
    for off in range(1, n_img):
        pl.semaphore_signal(barrier, inc=1, device_id={"img": img_peer(off)}, device_id_type=MESH)
    load_t = pltpu.make_async_copy(t_hbm, t_ref, loads.at[0])
    load_x = pltpu.make_async_copy(x_ref, imgs.at[me_t], loads.at[1])
    load_mask = pltpu.make_async_copy(mask_hbm, mask_ref, loads.at[2])
    for load in (load_t, load_x, load_mask):
        load.start()
    pl.semaphore_wait(barrier, n_tpl - 1 + n_img - 1)

    size = rows // parts

    def image_copy(src, block, k, way, to):
        piece = pl.ds(k * size, size)
        return pltpu.make_async_remote_copy(
            src_ref=src.at[piece], dst_ref=imgs.at[block, piece],
            send_sem=img_send.at[way, lax.div(block, 2), k],
            recv_sem=img_recv.at[block, k], device_id={"tpl": to}, device_id_type=MESH)

    right, left = me_t + 2, me_t - 2
    has_right, has_left = chip < chips - 1, chip > 0

    own_block = 2 * chip + core
    for k in range(parts):
        @pl.when(has_right)
        def _():
            image_copy(x_ref, own_block, k, 0, right).start()

        @pl.when(has_left)
        def _():
            image_copy(x_ref, own_block, k, 1, left).start()

        image_copy(x_ref, own_block, k, 2, sibling).start()

    for load in (load_t, load_x, load_mask):
        load.wait()
    tf = t_ref[...].astype(jnp.float32)
    sqn[...] = 0.5 * jnp.sum(tf * tf, axis=1, keepdims=True)
    acc[...] = jnp.zeros_like(acc)
    occ[...] = jnp.zeros_like(occ)

    def stat_copy(q, off):
        return pltpu.make_async_remote_copy(
            src_ref=st.at[q, me_t], dst_ref=st.at[q, me_t], send_sem=st_send.at[q, off],
            recv_sem=st_recv.at[q, off], device_id={"tpl": tpl_peer(off)}, device_id_type=MESH)

    def stat_arrival(q, off):
        src = lax.rem(me_t + n_tpl - off, n_tpl)
        return pltpu.make_async_remote_copy(
            src_ref=st.at[q, src], dst_ref=st.at[q, src], send_sem=st_send.at[q, off],
            recv_sem=st_recv.at[q, off], device_id={"tpl": tpl_peer(off)}, device_id_type=MESH)

    def pair_of(q):
        return imgs[pl.ds(2 * q, 2)].reshape(2 * rows, feats)

    class_count = power_ref.shape[0]
    tpl_rows = t_ref.shape[0]
    per_class = tpl_rows * n_tpl // class_count
    pair = 2 * rows
    first = me_t * tpl_rows
    for q in range(chips):
        allow[q] = mask_ref[:, q * pair:(q + 1) * pair]

    def inverse_temp(c):
        power = jnp.full((1, pair), power_ref[c], jnp.int32)
        return 0.5 * jnp.exp2(0.5 * power.astype(jnp.float32))

    if per_class % tpl_rows == 0:
        only = lax.div(first, per_class)
        beta = inverse_temp(only)

        def allowed_at(q):
            return allow[q, pl.ds(only, 1), :] > 0
    else:
        owner = lax.div(first + lax.broadcasted_iota(jnp.int32, (tpl_rows, pair), 0), per_class)
        beta = sum(jnp.where(owner == c, inverse_temp(c), 0.0) for c in range(class_count))

        def allowed_at(q):
            return sum(jnp.where(owner == c, allow[q, c:c + 1, :], 0) for c in range(class_count)) > 0

    def score(q):
        raw = lax.dot_general(
            t_ref[...], pair_of(q), (((1,), (1,)), ((), ())), preferred_element_type=jnp.float32)
        s = beta * (raw - sqn[...])
        allowed = allowed_at(q)
        top = jnp.max(jnp.where(allowed, s, floor_score), axis=0, keepdims=True)
        e = jnp.where(allowed, jnp.exp(s - top), 0.0)
        st[q, me_t, 0:1, :] = top
        st[q, me_t, 1:2, :] = jnp.sum(e, axis=0, keepdims=True)
        e_ref[q] = e
        for off in range(1, n_tpl):
            stat_copy(q, off).start()

    def wait_image(block, k):
        image_copy(imgs.at[block], block, k, 2, sibling).wait_recv()

    def relay(q, k, more, way, to):
        block = 2 * q + core
        wait_image(block, k)

        @pl.when(more)
        def _():
            image_copy(imgs.at[block], block, k, way, to).start()

        image_copy(imgs.at[block], block, k, 2, sibling).start()

    def finish(q):
        for k in range(parts):
            wait_image(2 * q + 1 - core, k)
        score(q)

    finish(chip)

    def arrive(d, carry):
        q_left, q_right = chip - d, chip + d
        for k in range(parts):
            @pl.when(q_left >= 0)
            def _():
                relay(q_left, k, has_right, 0, right)

            @pl.when(q_right < chips)
            def _():
                relay(q_right, k, has_left, 1, left)

        @pl.when(q_left >= 0)
        def _():
            finish(q_left)

        @pl.when(q_right < chips)
        def _():
            finish(q_right)

        return carry

    lax.fori_loop(1, chips, arrive, 0)

    def consume(q):
        for off in range(1, n_tpl):
            stat_arrival(q, off).wait_recv()
        tops = [st[q, j, 0:1, :] for j in range(n_tpl)]
        top = functools.reduce(jnp.maximum, tops)
        total = sum(st[q, j, 1:2, :] * jnp.exp(tops[j] - top) for j in range(n_tpl))
        factor = jnp.exp(st[q, me_t, 0:1, :] - top) / total
        post = e_ref[q] * factor
        occ[...] += jnp.sum(post, axis=1, keepdims=True)
        post_ref[q] = post.astype(jnp.bfloat16)
        le_row[q] = top + jnp.log(total)

    def middle(q, carry):
        consume(q)
        for j in range(n_img):
            part = slice(j * cols, (j + 1) * cols)
            block = imgs[pl.ds(2 * q, 2), :, part].reshape(2 * rows, cols)
            acc[:, part] += jnp.dot(post_ref[q], block, preferred_element_type=jnp.float32)
        return carry

    lax.fori_loop(1, chips - 1, middle, 0)
    ends = (0, chips - 1) if chips > 1 else (0,)
    for q in ends:
        consume(q)

    def occ_copy(off):
        return pltpu.make_async_remote_copy(
            src_ref=obuf, dst_ref=orecv.at[off], send_sem=oc_send.at[off],
            recv_sem=oc_recv.at[off], device_id={"img": img_peer(off)}, device_id_type=MESH)

    bits = [1 << k for k in range(n_img.bit_length() - 1)]
    groups = len(bits) if bits and tpl_rows % (16 * len(bits)) == 0 else 1
    depth = tpl_rows // groups
    orders = [bits[g:] + bits[:g] for g in range(groups)]

    def flip(mask):
        return me_i + sum(b - 2 * b * lax.rem(lax.div(me_i, b), 2) for b in bits if b & mask)

    def turn(g, mask):
        return next(r for r, b in enumerate(orders[g]) if b & mask)

    def band(g):
        return slice(g * depth, (g + 1) * depth)

    def sum_copy(g, mask):
        return pltpu.make_async_remote_copy(
            src_ref=sbuf.at[mask, band(g)], dst_ref=rbuf.at[mask, band(g)],
            send_sem=rs_send.at[g, mask], recv_sem=rs_recv.at[g, mask],
            device_id={"img": flip(orders[g][turn(g, mask)])}, device_id_type=MESH)

    def share(g, mask):
        part = pl.ds(pl.multiple_of(flip(mask) * cols, cols), cols)
        value = acc[band(g), part]
        for q in ends:
            block = imgs[2 * q:2 * q + 2, :, part].reshape(2 * rows, cols)
            value += jnp.dot(post_ref[q, band(g)], block, preferred_element_type=jnp.float32)
        return value

    def received(g, mask, rounds):
        value = 0.0
        for b in orders[g][:rounds]:
            sum_copy(g, b + mask).wait_recv()
            value += rbuf[b + mask, band(g)].astype(jnp.float32)
        return value

    for q in range(chips):
        le_ref[:, q * pair:(q + 1) * pair] = le_row[q]
    obuf[...] = jnp.transpose(jnp.broadcast_to(occ[...], (tpl_rows, 128)))[0:8]
    for off in range(1, n_img):
        occ_copy(off).start()
    masks = sorted(range(1, n_img), key=lambda mask: -mask.bit_count())
    mine = pl.ds(pl.multiple_of(me_i * cols, cols), cols)
    for r in range(len(bits)):
        for mask in masks:
            for g in range(groups):
                if turn(g, mask) == r:
                    value = share(g, mask)
                    sbuf[mask, band(g)] = (value + received(g, mask, r)).astype(jnp.bfloat16)
                    sum_copy(g, mask).start()
        if r == 0:
            for g in range(groups):
                own[band(g)] = share(g, 0) + t_ref[band(g), mine].astype(jnp.float32)
            occ_row = obuf[...]
            for off in range(1, n_img):
                occ_copy(off).wait_recv()
                occ_row += orecv[off]
            occ_col = jnp.transpose(jnp.broadcast_to(occ_row[0:1], (128, tpl_rows)))[:, 0:1]
            occ[...] = occ_col + 1.0
    for g in range(groups):
        out_ref[band(g)] = (own[band(g)] + received(g, 0, len(bits))) / occ[band(g)]

    for off in range(1, n_img):
        occ_copy(off).wait_send()
        for g in range(groups):
            sum_copy(g, off).wait_send()

    def drain(q, carry):
        block = 2 * q + core
        for k in range(parts):
            @pl.when(jnp.logical_and(has_right, q <= chip))
            def _():
                image_copy(imgs.at[block], block, k, 0, right).wait_send()

            @pl.when(jnp.logical_and(has_left, q >= chip))
            def _():
                image_copy(imgs.at[block], block, k, 1, left).wait_send()

            image_copy(imgs.at[block], block, k, 2, sibling).wait_send()
        for off in range(1, n_tpl):
            stat_copy(q, off).wait_send()
        return carry

    lax.fori_loop(0, chips, drain, 0)


def emit(new_ref, evidence_ref, new_out, evidence_out):
    new_out[...] = new_ref[...]
    evidence_out[...] = evidence_ref[...].reshape(evidence_out.shape)


def solution(mesh):
    n_img, n_tpl = mesh.shape["img"], mesh.shape["tpl"]
    chips = n_tpl // 2

    def per_device(images, templates, class_exponent, class_mask):
        rows, feats = images.shape
        tpl_rows = templates.shape[0]
        cols = feats // n_img
        class_count = class_exponent.shape[0]
        parts = max(c for c in (4, 3, 2, 1) if rows % (16 * c) == 0 or c == 1)
        dma = pltpu.SemaphoreType.DMA
        vmem = pl.BlockSpec(memory_space=pltpu.VMEM)
        far = pl.BlockSpec(memory_space=pl.ANY)
        new, evidence = pl.pallas_call(
            functools.partial(kernel, n_img, n_tpl, parts),
            out_shape=(
                jax.ShapeDtypeStruct((tpl_rows, cols), jnp.float32),
                jax.ShapeDtypeStruct((1, n_tpl * rows), jnp.float32),
            ),
            in_specs=[far, far, pl.BlockSpec(memory_space=pltpu.SMEM), far],
            out_specs=(vmem, vmem),
            scratch_shapes=[
                pltpu.VMEM((tpl_rows, feats), jnp.bfloat16),
                pltpu.VMEM((class_count, n_tpl * rows), jnp.int32),
                dma((3,)),
                pltpu.VMEM((n_tpl, rows, feats), jnp.bfloat16),
                pltpu.VMEM((chips, class_count, 2 * rows), jnp.int32),
                pltpu.VMEM((chips, 1, 2 * rows), jnp.float32),
                pltpu.VMEM((chips, tpl_rows, 2 * rows), jnp.float32),
                pltpu.VMEM((chips, tpl_rows, 2 * rows), jnp.bfloat16),
                pltpu.VMEM((chips, n_tpl, 2, 2 * rows), jnp.float32),
                pltpu.VMEM((tpl_rows, feats), jnp.float32),
                pltpu.VMEM((tpl_rows, cols), jnp.float32),
                pltpu.VMEM((n_img, tpl_rows, cols), jnp.bfloat16),
                pltpu.VMEM((n_img, tpl_rows, cols), jnp.bfloat16),
                pltpu.VMEM((tpl_rows, 1), jnp.float32),
                pltpu.VMEM((tpl_rows, 1), jnp.float32),
                pltpu.VMEM((8, tpl_rows), jnp.float32),
                pltpu.VMEM((n_img, 8, tpl_rows), jnp.float32),
                dma((3, chips, parts)),
                dma((n_tpl, parts)),
                dma((chips, n_tpl)),
                dma((chips, n_tpl)),
                dma((n_img, n_img)),
                dma((n_img, n_img)),
                dma((n_img,)),
                dma((n_img,)),
            ],
            compiler_params=pltpu.CompilerParams(
                collective_id=0, has_side_effects=True, vmem_limit_bytes=60 * 1024 * 1024),
        )(images, templates, class_exponent, class_mask.T)
        return pl.pallas_call(
            emit,
            out_shape=(
                jax.ShapeDtypeStruct(new.shape, jnp.float32),
                jax.ShapeDtypeStruct((n_tpl * rows,), jnp.float32),
            ),
            in_specs=[vmem] * 2,
            out_specs=(vmem, vmem),
        )(new, evidence)

    in_specs = (P(("img", "tpl"), None), P("tpl", None), P(), P("img", None))
    out_specs = (P("tpl", "img"), P("img"))
    return jax.shard_map(
        per_device, mesh=mesh, in_specs=in_specs, out_specs=out_specs, check_vma=False
    )
```
